512 devices in a mesh: rep: 128 (over y, z, core), tp: 4 (over x).
Axes of the slice: x: 4, y: 8, z: 8, core: 2. Of those that a mesh axis runs over, the one named last changes fastest.
Arguments:
- gradients: bfloat16 [128, 1024, 1024], P('rep', None, 'tp'), may hold values from -24 to 24
- feedback: float32 [128, 1024, 1024], P('rep', None, 'tp'), may hold values from -4 to 4
- warm_factor: float32 [1024, 32], P('tp'), may hold values from -0.1875 to 0.1875
- momentum: float32 [1024, 1024], P('rep', 'tp'), may hold values from -3 to 3
- master_owned: float32 [1024, 1024], P('rep', 'tp'), may hold values from -4 to 4
- vector_grads: float32 [128, 2560], P('rep'), may hold values from -6 to 6
- vector_params: float32 [2560], replicated, may hold values from 0.5 to 1.5
- vector_momentum: float32 [2560], replicated, may hold values from -3 to 3
Outputs:
- new_feedback: float32 [128, 1024, 1024], P('rep', None, 'tp')
- new_momentum: float32 [1024, 1024], P('rep', 'tp')
- new_master: float32 [1024, 1024], P('rep', 'tp')
- weight: bfloat16 [1024, 1024], P(None, 'tp')
- new_vector_params: float32 [2560], replicated
- new_vector_momentum: float32 [2560], replicated
The draws below stay inside these ranges and needn't reach their ends.
All inputs are finite; a program needn't handle non-finite values.
Results may differ from the reference program's by a relative error of at most 0.0049.
Values may be sent and summed in bfloat16 or wider, within the bound.
No kernel may reach another device: no remote copies, remote signals or barrier semaphores. Data moves between devices by JAX's collectives and lax.ppermute only.
A program may use at most 64 MiB of HBM per device.

```python
import jax
import jax.numpy as jnp
from jax import lax

D = 1024
RANK = 32
REPLICAS = 128
VEC = 2560


def with_spikes(drawn, rng, source, target, shards_of, factor):
    owner, partner = [(jnp.arange(drawn.shape[dim]) // (drawn.shape[dim] // shards_of)).reshape([-1 if axis == dim else 1 for axis in range(drawn.ndim)]) for dim in (source, target)]
    chosen = jax.random.permutation(rng, shards_of)[partner]
    strong = (owner == chosen) | (owner == (partner + shards_of // 2) % shards_of)
    return jnp.where(strong, factor * drawn, drawn)


def block_scale(own_key, extent, cuts, low, high):
    def one(position, shards_of):
        steps = jax.random.uniform(jax.random.fold_in(jax.random.fold_in(own_key, 6), position), (shards_of,), jnp.float32, low / len(cuts), high / len(cuts))
        return jnp.repeat(jnp.exp(steps), extent[position] // shards_of).reshape((-1,) + (1,) * (len(extent) - position - 1))

    gain = one(*cuts[0])
    for cut in cuts[1:]:
        gain = gain * one(*cut)
    return gain


def normal_values(own_key, shape, width, bound, cuts=(), kind=jnp.bfloat16):
    factor_of = block_scale(own_key, shape, cuts, -0.22, 0.18) if cuts else 1.0
    drawn = jax.random.normal(own_key, shape, jnp.float32) * width * factor_of
    return jnp.minimum(jnp.maximum(drawn, -bound), bound).astype(kind)


def noise_with(rng, shape, width, reach, cuts, heavy, kind=jnp.bfloat16):
    array = width * jax.random.normal(rng, shape, jnp.float32)
    if cuts:
        array = array * block_scale(rng, shape, cuts, -0.22, 0.18)
    return jnp.clip(with_spikes(array, jax.random.fold_in(rng, 3), *heavy), -reach, reach).astype(kind)


def setup_inputs(seed: int = 0) -> dict:
    key_of = jax.random.split(jax.random.key(seed), 9)
    gradients = noise_with(key_of[0], (REPLICAS, D, D), 1.0, 24.0, ((0, 128), (2, 4)), (0, 1, 128, 5.5))
    feedback = normal_values(key_of[1], (REPLICAS, D, D), 0.5, 4.0, ((0, 128), (2, 4)), jnp.float32)
    warm_factor = normal_values(key_of[2], (D, RANK), D ** -0.5, 0.1875, ((0, 4),), jnp.float32)
    momentum = normal_values(key_of[3], (D, D), 0.3, 3.0, ((0, 128), (1, 4)), jnp.float32)
    master_owned = normal_values(key_of[4], (D, D), 0.5, 4.0, ((0, 128), (1, 4)), jnp.float32)
    vector_grads = normal_values(key_of[5], (REPLICAS, VEC), 1.0, 6.0, ((0, 128),), jnp.float32)
    vector_params = jnp.clip(1.0 + 0.1 * jax.random.normal(key_of[6], (VEC,), jnp.float32), 0.5, 1.5)
    vector_momentum = normal_values(key_of[7], (VEC,), 0.3, 3.0, (), jnp.float32)
    return dict(gradients=gradients, feedback=feedback, warm_factor=warm_factor, momentum=momentum, master_owned=master_owned, vector_grads=vector_grads, vector_params=vector_params, vector_momentum=vector_momentum)


PRECISE = lax.Precision.HIGHEST
MOMENTUM_RATE = 0.9
LEARN_RATE = 0.5

def combined_member(gradients, feedback, member):
    return gradients[member].astype(jnp.float32) + feedback[member]

def left_product(gradients, feedback, factor):

    def accumulate(total, member):
        part = jnp.dot(combined_member(gradients, feedback, member), factor, precision=PRECISE)
        return (total + part, None)
    total, unused = lax.scan(accumulate, jnp.zeros((D, RANK), jnp.float32), jnp.arange(REPLICAS, dtype=jnp.int32))
    return total

def right_product(gradients, feedback, factor):

    def accumulate(total, member):
        part = jnp.dot(combined_member(gradients, feedback, member).T, factor, precision=PRECISE)
        return (total + part, None)
    total, unused = lax.scan(accumulate, jnp.zeros((D, RANK), jnp.float32), jnp.arange(REPLICAS, dtype=jnp.int32))
    return total

def orthonormal(left):
    gram = jnp.dot(left.T, left, precision=PRECISE)
    lower = jnp.linalg.cholesky(gram)
    return jax.scipy.linalg.solve_triangular(lower, left.T, lower=True).T

def reference(gradients, feedback, warm_factor, momentum, master_owned, vector_grads, vector_params, vector_momentum):
    left_one = left_product(gradients, feedback, warm_factor)
    ortho_one = orthonormal(left_one)
    right_one = right_product(gradients, feedback, ortho_one)
    left_two = left_product(gradients, feedback, right_one)
    ortho_two = orthonormal(left_two)
    right_two = right_product(gradients, feedback, ortho_two)
    approx = jnp.dot(ortho_two, right_two.T, precision=PRECISE) / REPLICAS
    new_feedback = gradients.astype(jnp.float32) + feedback - approx[None]
    new_momentum = MOMENTUM_RATE * momentum + approx
    new_master = master_owned - LEARN_RATE * new_momentum
    weight = new_master.astype(jnp.bfloat16)
    vector_sum = jnp.sum(vector_grads, axis=0)
    new_vector_momentum = MOMENTUM_RATE * vector_momentum + vector_sum / REPLICAS
    new_vector_params = vector_params - LEARN_RATE * new_vector_momentum
    return (new_feedback, new_momentum, new_master, weight, new_vector_params, new_vector_momentum)
```

```python
import jax
import jax.numpy as jnp
from jax import lax
from jax.sharding import Mesh
from jax.sharding import PartitionSpec as P

REP = ("y", "z", "c")
CHIPS = ("y", "z")
PRECISE = lax.Precision.HIGHEST
MOMENTUM_RATE = 0.9
LEARN_RATE = 0.5
F32 = jnp.float32
BF16 = jnp.bfloat16
SWAP = ((0, 1), (1, 0))


def split(values):
    high = values.astype(BF16)
    return high, (values - high.astype(F32)).astype(BF16)


def exchange(array, axis):
    return lax.all_to_all(array, axis, 0, 0, tiled=True)


def sent_to_all(array, axis):
    peers = lax.axis_size(axis)
    return exchange(jnp.broadcast_to(array, (peers, *array.shape)), axis)


def factor_of(left):
    return jnp.linalg.cholesky(jnp.dot(left.T, left, precision=PRECISE))


def solved(lower, left):
    return jax.scipy.linalg.solve_triangular(lower, left.T, lower=True).T


def shards(
    gradients,
    feedback,
    warm_factor,
    momentum,
    master_owned,
    vector_grads,
    vector_params,
    vector_momentum,
):
    replicas = lax.axis_size(REP)
    chips = lax.axis_size(CHIPS)
    core = lax.axis_index("c")
    rows, cols = gradients.shape[1:]
    owned = momentum.shape[0]
    rank = warm_factor.shape[1]
    combined = gradients[0].astype(F32) + feedback[0]

    by_owner = combined.reshape(chips, 2, owned, cols)
    part = vector_grads.shape[1] // replicas
    vector_parts = vector_grads.reshape(2, chips, 1, part)
    lanes = 128

    def packed(side):
        block = lax.dynamic_index_in_dim(by_owner, side, 1, keepdims=False)
        values = lax.dynamic_index_in_dim(vector_parts, side, 0, keepdims=False)
        high, low = split(values)
        extra = jnp.concatenate([high, low], 1).astype(F32)
        extra = jnp.pad(extra, ((0, 0), (0, owned - 2), (0, lanes - part)))
        return jnp.concatenate([block, extra], 2)

    other = lax.ppermute(packed(1 - core).astype(BF16), "c", SWAP)
    paired = packed(core) + other.astype(F32)
    pair_vector = paired[:, 0, cols : cols + part] + paired[:, 1, cols : cols + part]
    high, low = split(pair_vector)
    sending = jnp.concatenate([paired[:, :, :cols].astype(BF16), jnp.pad(jnp.stack([high, low], 1), ((0, 0), (0, owned - 2), (0, lanes - part)))], 2)
    arrived = exchange(sending, CHIPS).astype(F32).sum(0)
    block = arrived[:, :cols]
    own_vector = arrived[0, cols : cols + part] + arrived[1, cols : cols + part]

    left_rows = jnp.dot(block, warm_factor, precision=PRECISE)
    left_rows = sent_to_all(left_rows, "tp").sum(0)

    base = master_owned - LEARN_RATE * MOMENTUM_RATE * momentum
    left_high, left_low = split(left_rows)
    high, low = split(own_vector)
    vector_lanes = jnp.pad(jnp.stack([high, low], 0), ((0, owned - 2), (0, lanes - 2 * rank - part)))
    shared = jnp.concatenate([block.astype(BF16), left_high, left_low, vector_lanes, base.astype(BF16)], 1)
    near = sent_to_all(shared, CHIPS)
    far = lax.ppermute(near, "c", SWAP)
    whole = jnp.where(core == 0, jnp.stack([near, far], 1), jnp.stack([far, near], 1))
    flat = whole.reshape(rows, -1)
    summed = flat[:, :cols].astype(F32)
    left_one = flat[:, cols : cols + rank].astype(F32) + flat[:, cols + rank : cols + 2 * rank].astype(F32)
    base_rows = flat[:, cols + lanes :].astype(F32)
    at = cols + 2 * rank
    vector_sum = (whole[:, :, 0, at : at + part].astype(F32) + whole[:, :, 1, at : at + part].astype(F32)).swapaxes(0, 1).reshape(-1)

    right = lax.dot_general(summed, left_one, (((0,), (0,)), ((), ())), precision=PRECISE)
    partial = jnp.dot(summed, right, precision=PRECISE).astype(BF16)
    lower_one = factor_of(left_one)
    left_two = sent_to_all(partial, "tp").astype(F32).sum(0)
    left_two = solved(lower_one, left_two)
    ortho_two = solved(factor_of(left_two), left_two)
    right_two = lax.dot_general(summed, ortho_two, (((0,), (0,)), ((), ())), precision=PRECISE)
    approx = jnp.dot(ortho_two, right_two.T, precision=PRECISE) / replicas

    new_feedback = (combined - approx)[None]
    row_start = lax.axis_index(REP) * owned
    owned_approx = lax.dynamic_slice_in_dim(approx, row_start, owned, 0)
    new_momentum = MOMENTUM_RATE * momentum + owned_approx
    new_master = master_owned - LEARN_RATE * new_momentum
    weight = (base_rows - LEARN_RATE * approx).astype(BF16)
    new_vector_momentum = MOMENTUM_RATE * vector_momentum + vector_sum / replicas
    new_vector_params = vector_params - LEARN_RATE * new_vector_momentum
    return (new_feedback, new_momentum, new_master, weight, new_vector_params, new_vector_momentum)


def solution(mesh):
    finer = Mesh(mesh.devices.reshape(8, 8, 2, mesh.shape["tp"]), ("y", "z", "c", "tp"))
    in_specs = (
        P(REP, None, "tp"),
        P(REP, None, "tp"),
        P("tp", None),
        P(REP, "tp"),
        P(REP, "tp"),
        P(REP, None),
        P(),
        P(),
    )
    out_specs = (P(REP, None, "tp"), P(REP, "tp"), P(REP, "tp"), P(None, "tp"), P(), P())
    return jax.shard_map(
        shards, mesh=finer, in_specs=in_specs, out_specs=out_specs, check_vma=False
    )
```

```python
import functools

import jax
import jax.numpy as jnp
from jax import lax
from jax.experimental import pallas as pl
from jax.experimental.pallas import tpu as pltpu
from jax.sharding import Mesh
from jax.sharding import PartitionSpec as P

REP = ("y", "z", "c")
CHIPS = ("y", "z")
PRECISE = lax.Precision.HIGHEST
MOMENTUM_RATE = 0.9
LEARN_RATE = 0.5
F32 = jnp.float32
BF16 = jnp.bfloat16
SWAP = ((0, 1), (1, 0))
LANES = 128
PIVOTS = 8
CHUNKS = 4
VMEM = pl.BlockSpec(memory_space=pltpu.VMEM)
SMEM = pl.BlockSpec(memory_space=pltpu.SMEM)
ANY = pl.BlockSpec(memory_space=pl.ANY)
SMALL = pltpu.CompilerParams(vmem_limit_bytes=8 << 20)
LARGE = pltpu.CompilerParams(vmem_limit_bytes=20 << 20)


def split(values):
    high = values.astype(BF16)
    return high, (values - high.astype(F32)).astype(BF16)


def exchange(array, axis):
    return lax.all_to_all(array, axis, 0, 0, tiled=True)


def product(left, right, dims, precision=None):
    return lax.dot_general(left, right, (dims, ((), ())), precision=precision, preferred_element_type=F32)


def times_exact(factor, exact, dims):
    both = product(jnp.concatenate(split(factor), 0), exact, dims)
    rows = factor.shape[0]
    return both[:rows] + both[rows:]


def lower_inverse(gram):
    n = gram.shape[0]
    lane = lax.broadcasted_iota(jnp.int32, (n, LANES), 1)
    row = lax.broadcasted_iota(jnp.int32, (n, LANES), 0)
    eye = jnp.where(lane == row + n, 1.0, 0.0).astype(F32)
    work = jnp.concatenate([gram, jnp.zeros((n, LANES - n), F32)], 1) + eye
    inverses = []
    for first in range(0, n, PIVOTS):
        cols = [jnp.broadcast_to(work[:, first + j : first + j + 1], (n, LANES)) for j in range(PIVOTS)]
        lines = [work[first + j : first + j + 1, :] for j in range(PIVOTS)]
        for j in range(PIVOTS):
            at = first + j
            inverse = 1.0 / cols[j][at : at + 1, :]
            inverses.append(inverse)
            scaled = lines[j] * inverse
            below = jnp.where(row > at, cols[j], 0.0)
            for m in range(j + 1, PIVOTS):
                lines[m] = lines[m] - cols[j][first + m : first + m + 1, :] * scaled
                cols[m] = cols[m] - below * (cols[m][at : at + 1, :] * inverse)
            work = work - below * scaled
    return (work * jnp.sqrt(jnp.concatenate(inverses, 0)))[:, n : 2 * n]


def gram_inverse(left):
    return lower_inverse(product(left, left, ((1,), (1,)), PRECISE))


def share_kernel(arrived, momentum, master, out):
    cols = momentum.shape[1]
    total = jnp.sum(arrived[...].astype(F32), axis=0)
    high, low = split(total[0:1, cols:] + total[1:2, cols:])
    row = lax.broadcasted_iota(jnp.int32, (total.shape[0], LANES), 0)
    vector = jnp.where(row == 0, high.astype(F32), jnp.where(row == 1, low.astype(F32), 0.0))
    base = master[...] - LEARN_RATE * MOMENTUM_RATE * momentum[...]
    shared = jnp.concatenate([total[:, :cols], vector, base], 1).astype(BF16)
    out[...] = jnp.broadcast_to(shared, out.shape)


def matrix_of(ref, cols):
    return ref[:, :, :cols].reshape(-1, cols)


def left_kernel(near, factor, out):
    cols = factor.shape[0]
    left = times_exact(factor[...].T, matrix_of(near, cols), ((1,), (1,)))
    out[...] = jnp.broadcast_to(left.astype(BF16), out.shape)


def left_sum(place, arrived):
    tp = arrived.shape[0] // 2
    core = place[0]

    def half(side):
        return jnp.sum(arrived[pl.ds(side * tp, tp)].astype(F32), axis=0)

    return half(core), half(1 - core)


def power_kernel(place, arrived, near, far, out, vector):
    cols = near.shape[2] * 2 // 5
    core = place[0]
    for side, ref in ((core, near), (1 - core, far)):
        vector[side] = ref[:, 0, cols : cols + LANES].astype(F32) + ref[:, 1, cols : cols + LANES].astype(F32)
    own, other = left_sum(place, arrived)
    near_matrix, far_matrix = matrix_of(near, cols), matrix_of(far, cols)
    right = times_exact(own, near_matrix, ((1,), (0,))) + times_exact(other, far_matrix, ((1,), (0,)))
    half = own.shape[1]
    for side, matrix in enumerate((near_matrix, far_matrix)):
        left = times_exact(right, matrix, ((1,), (1,))).astype(BF16)
        out[:, :, side * half : (side + 1) * half] = jnp.broadcast_to(left, (out.shape[0], *left.shape))


def factor_kernel(place, arrived, after, out):
    del after
    own, other = left_sum(place, arrived)
    out[...] = gram_inverse(jnp.concatenate([own, other], 1))


def finish_kernel(
    place,
    parts,
    inverse_one,
    near,
    far,
    gradients,
    feedback,
    momentum,
    master,
    new_feedback,
    weight,
    new_momentum,
    new_master,
    ortho_terms,
    right_terms,
    feedback_buffer,
    weight_buffer,
    base,
    owned,
    sems,
    *,
    replicas,
):
    core, chip = place[0], place[1]
    chips, pair, cols = feedback.shape
    rows = pair // 2
    half = chips * rows
    for side, ref in ((core, near), (1 - core, far)):
        base[side] = ref[:, :, cols + LANES :]
    left = product(inverse_one[...], jnp.sum(parts[...].astype(F32), axis=0), ((1,), (0,)), PRECISE)
    ortho = product(gram_inverse(left), left, ((1,), (0,)), PRECISE)
    right = times_exact(ortho[:, :half], matrix_of(near, cols), ((1,), (0,)))
    right += times_exact(ortho[:, half:], matrix_of(far, cols), ((1,), (0,)))
    right_high, right_low = split(right / replicas)
    right_terms[...] = jnp.concatenate([right_high, right_low, right_high], 0)
    for side, start in enumerate((core * half, (1 - core) * half)):
        high, low = split(ortho[:, side * half : (side + 1) * half])
        ortho_terms[:, pl.ds(pl.multiple_of(start, LANES), half)] = jnp.concatenate([high, high, low], 0)
    step = chips // CHUNKS
    copies = []
    for chunk in range(CHUNKS):
        span = slice(chunk * step, (chunk + 1) * step)
        sides = []
        for side in range(2):
            at = side * half + chunk * step * rows
            terms = ortho_terms[:, at : at + step * rows]
            sides.append(product(terms, right_terms[...], ((0,), (0,))).reshape(step, rows, cols))
        approx = jnp.concatenate(sides, 1)
        owned[:, span] = jnp.stack(sides, 0)
        feedback_buffer[span] = gradients[span].astype(F32) + feedback[span] - approx
        kept = [base[side, span].astype(F32) for side in range(2)]
        weight_buffer[span] = (jnp.concatenate(kept, 1) - LEARN_RATE * approx).astype(BF16)
        for which, (source, target) in enumerate(((feedback_buffer, new_feedback), (weight_buffer, weight))):
            copy = pltpu.make_async_copy(source.at[span], target.at[span], sems.at[chunk, which])
            copy.start()
            copies.append(copy)
    moved = MOMENTUM_RATE * momentum[...] + owned[core, chip]
    new_momentum[...] = moved
    new_master[...] = master[...] - LEARN_RATE * moved
    for copy in copies:
        copy.wait()


def shards(
    gradients,
    feedback,
    warm_factor,
    momentum,
    master_owned,
    vector_grads,
    vector_params,
    vector_momentum,
):
    replicas = lax.axis_size(REP)
    chips = lax.axis_size(CHIPS)
    tp = lax.axis_size("tp")
    core = lax.axis_index("c")
    rows, cols = gradients.shape[1:]
    owned = momentum.shape[0]
    rank = warm_factor.shape[1]
    half = rows // 2
    place = jnp.stack([core, lax.axis_index(CHIPS)]).astype(jnp.int32)
    by_pair = (chips, 2 * owned, cols)

    combined = gradients[0].astype(F32) + feedback[0]
    by_owner = combined.reshape(chips, 2, owned, cols)
    part = vector_grads.shape[1] // replicas
    vector_parts = vector_grads.reshape(2, chips, 1, part)

    def two_rows(values):
        pair = jnp.concatenate([v.astype(F32) for v in split(values)], 1)
        return jnp.pad(pair, ((0, 0), (0, owned - 2), (0, LANES - part)))

    def packed(side):
        block = lax.dynamic_index_in_dim(by_owner, side, 1, keepdims=False)
        return block, lax.dynamic_index_in_dim(vector_parts, side, 0, keepdims=False)

    block, vector = packed(1 - core)
    other = lax.ppermute(jnp.concatenate([block, two_rows(vector)], 2).astype(BF16), "c", SWAP).astype(F32)
    block, vector = packed(core)
    block = block + other[:, :, :cols]
    vector = vector + other[:, 0:1, cols : cols + part] + other[:, 1:2, cols : cols + part]
    arrived = exchange(jnp.concatenate([block, two_rows(vector)], 2).astype(BF16), CHIPS)

    shared_cols = 2 * cols + LANES
    shared = pl.pallas_call(
        share_kernel,
        out_shape=jax.ShapeDtypeStruct((chips, owned, shared_cols), BF16),
        in_specs=[VMEM] * 3,
        out_specs=VMEM,
        compiler_params=SMALL,
        name="share",
    )(arrived, momentum, master_owned)
    near = exchange(shared, CHIPS)
    far = lax.ppermute(near, "c", SWAP)
    left = pl.pallas_call(
        left_kernel,
        out_shape=jax.ShapeDtypeStruct((2 * tp, rank, half), BF16),
        in_specs=[VMEM] * 2,
        out_specs=VMEM,
        compiler_params=SMALL,
        name="left",
    )(near, warm_factor)
    left = exchange(left, ("c", "tp"))
    parts, vector = pl.pallas_call(
        power_kernel,
        out_shape=(
            jax.ShapeDtypeStruct((tp, rank, rows), BF16),
            jax.ShapeDtypeStruct((2, chips, LANES), F32),
        ),
        in_specs=[SMEM] + [VMEM] * 3,
        out_specs=(VMEM, VMEM),
        compiler_params=SMALL,
        name="power",
    )(place, left, near, far)
    parts = exchange(parts, "tp")
    inverse_one = pl.pallas_call(
        factor_kernel,
        out_shape=jax.ShapeDtypeStruct((rank, rank), F32),
        in_specs=[SMEM, VMEM, ANY],
        out_specs=VMEM,
        compiler_params=SMALL,
        name="factor",
    )(place, left, vector)
    vector_sum = vector[:, :, :part].reshape(-1)

    new_feedback, weight, new_momentum, new_master = pl.pallas_call(
        functools.partial(finish_kernel, replicas=replicas),
        out_shape=(
            jax.ShapeDtypeStruct(by_pair, F32),
            jax.ShapeDtypeStruct(by_pair, BF16),
            jax.ShapeDtypeStruct(momentum.shape, F32),
            jax.ShapeDtypeStruct(momentum.shape, F32),
        ),
        in_specs=[SMEM] + [VMEM] * 8,
        out_specs=(ANY, ANY, VMEM, VMEM),
        scratch_shapes=[
            pltpu.VMEM((3 * rank, rows), BF16),
            pltpu.VMEM((3 * rank, cols), BF16),
            pltpu.VMEM(by_pair, F32),
            pltpu.VMEM(by_pair, BF16),
            pltpu.VMEM((2, chips, owned, cols), BF16),
            pltpu.VMEM((2, chips, owned, cols), F32),
            pltpu.SemaphoreType.DMA((CHUNKS, 2)),
        ],
        compiler_params=LARGE,
        name="finish",
    )(
        place,
        parts,
        inverse_one,
        near,
        far,
        gradients.reshape(by_pair),
        feedback.reshape(by_pair),
        momentum,
        master_owned,
    )
    new_vector_momentum = MOMENTUM_RATE * vector_momentum + vector_sum / replicas
    new_vector_params = vector_params - LEARN_RATE * new_vector_momentum
    return (
        new_feedback.reshape(feedback.shape),
        new_momentum,
        new_master,
        weight.reshape(rows, cols),
        new_vector_params,
        new_vector_momentum,
    )


def solution(mesh):
    finer = Mesh(mesh.devices.reshape(8, 8, 2, mesh.shape["tp"]), ("y", "z", "c", "tp"))
    in_specs = (
        P(REP, None, "tp"),
        P(REP, None, "tp"),
        P("tp", None),
        P(REP, "tp"),
        P(REP, "tp"),
        P(REP, None),
        P(),
        P(),
    )
    out_specs = (P(REP, None, "tp"), P(REP, "tp"), P(REP, "tp"), P(None, "tp"), P(), P())
    return jax.shard_map(
        shards, mesh=finer, in_specs=in_specs, out_specs=out_specs, check_vma=False
    )
```

```python
import functools

import jax
import jax.numpy as jnp
from jax import lax
from jax.experimental import pallas as pl
from jax.experimental.pallas import tpu as pltpu
from jax.sharding import Mesh
from jax.sharding import PartitionSpec as P

REP = ("y", "z", "c")
CHIPS = ("y", "z")
PRECISE = lax.Precision.HIGHEST
MOMENTUM_RATE = 0.9
LEARN_RATE = 0.5
F32 = jnp.float32
BF16 = jnp.bfloat16
SWAP = ((0, 1), (1, 0))
LANES = 128
PIVOTS = 8
CHUNKS = 4
TP = 4
VMEM = pl.BlockSpec(memory_space=pltpu.VMEM)
SMEM = pl.BlockSpec(memory_space=pltpu.SMEM)
ANY = pl.BlockSpec(memory_space=pl.ANY)
SMALL = pltpu.CompilerParams(vmem_limit_bytes=8 << 20)
LARGE = pltpu.CompilerParams(vmem_limit_bytes=20 << 20)


def split(values):
    high = values.astype(BF16)
    return high, (values - high.astype(F32)).astype(BF16)


def exchange(array, axis):
    return lax.all_to_all(array, axis, 0, 0, tiled=True)


def product(left, right, dims, precision=None):
    return lax.dot_general(left, right, (dims, ((), ())), precision=precision, preferred_element_type=F32)


def times_exact(factor, exact, dims):
    both = product(jnp.concatenate(split(factor), 0), exact, dims)
    rows = factor.shape[0]
    return both[:rows] + both[rows:]


def lower_inverse(gram):
    n = gram.shape[0]
    lane = lax.broadcasted_iota(jnp.int32, (n, LANES), 1)
    row = lax.broadcasted_iota(jnp.int32, (n, LANES), 0)
    eye = jnp.where(lane == row + n, 1.0, 0.0).astype(F32)
    work = jnp.concatenate([gram, jnp.zeros((n, LANES - n), F32)], 1) + eye
    inverses = []
    for first in range(0, n, PIVOTS):
        cols = [jnp.broadcast_to(work[:, first + j : first + j + 1], (n, LANES)) for j in range(PIVOTS)]
        lines = [work[first + j : first + j + 1, :] for j in range(PIVOTS)]
        for j in range(PIVOTS):
            at = first + j
            inverse = 1.0 / cols[j][at : at + 1, :]
            inverses.append(inverse)
            scaled = lines[j] * inverse
            below = jnp.where(row > at, cols[j], 0.0)
            for m in range(j + 1, PIVOTS):
                lines[m] = lines[m] - cols[j][first + m : first + m + 1, :] * scaled
                cols[m] = cols[m] - below * (cols[m][at : at + 1, :] * inverse)
            work = work - below * scaled
    return (work * jnp.sqrt(jnp.concatenate(inverses, 0)))[:, n : 2 * n]


def gram_inverse(left):
    return lower_inverse(product(left, left, ((1,), (1,)), PRECISE))


def quarter_of(place, vector):
    count = vector.shape[0] // TP
    rows = [vector[place[2] * count + j] for j in range(count)]
    return jnp.concatenate(rows + [jnp.zeros((8 - count, LANES), F32)], 0)


def half_of(side, gradients, feedback, narrow, wide, sems, store):
    step = gradients.shape[0] // CHUNKS
    spans = [slice(chunk * step, (chunk + 1) * step) for chunk in range(CHUNKS)]
    copies = []
    for chunk, span in enumerate(spans):
        for which, (source, target) in enumerate(((gradients, narrow), (feedback, wide))):
            copy = pltpu.make_async_copy(source.at[span, side], target.at[span], sems.at[chunk, which])
            copy.start()
            copies.append(copy)
    for chunk, span in enumerate(spans):
        copies[2 * chunk].wait()
        copies[2 * chunk + 1].wait()
        store(span, narrow[span].astype(F32) + wide[span])


def send_kernel(place, gradients, feedback, vector, out, narrow, wide, sems):
    def store(span, values):
        out[span] = values.astype(BF16)

    out[gradients.shape[0]] = jnp.concatenate(split(quarter_of(place, vector)), 1)
    half_of(1 - place[0], gradients, feedback, narrow, wide, sems, store)


def keep_kernel(place, gradients, feedback, after, out, narrow, wide, sems):
    del after

    def store(span, values):
        out[span] = values

    half_of(place[0], gradients, feedback, narrow, wide, sems, store)


def pair_kernel(kept, received, out):
    out[...] = (kept[...] + received[: kept.shape[0]].astype(F32)).astype(BF16)


def packed_rows(rows):
    high, low = split(rows)
    return jnp.concatenate([high.astype(F32), low.astype(F32), jnp.zeros((2, LANES), F32)], 0)


def share_kernel(place, arrived, received, vector, momentum, master, out):
    total = jnp.sum(arrived[...].astype(F32), axis=0)
    other = received[received.shape[0] - 1].astype(F32)
    quarter = quarter_of(place, vector) + other[:, :LANES] + other[:, LANES:]
    rows = jnp.where(place[0] == 0, quarter[0:3], quarter[3:6])
    base = master[...] - LEARN_RATE * MOMENTUM_RATE * momentum[...]
    shared = jnp.concatenate([total, packed_rows(rows), base], 1).astype(BF16)
    out[...] = jnp.broadcast_to(shared, out.shape)


def matrix_of(ref, cols):
    return ref[:, :, :cols].reshape(-1, cols)


def left_kernel(near, factor, out):
    cols, _ = factor.shape
    left = times_exact(factor[...].T, matrix_of(near, cols), ((1,), (1,)))
    spread = jnp.sum(near[:, :, cols : cols + LANES].astype(F32), axis=0)
    rows = packed_rows(spread[0:3] + spread[3:6])
    rows = jnp.concatenate([rows, jnp.zeros((8, left.shape[1] - LANES), F32)], 1)
    both = jnp.concatenate([left, rows], 0).astype(BF16)
    out[...] = jnp.broadcast_to(both, out.shape)


def left_sum(place, arrived):
    tp = arrived.shape[0] // 2
    rank = arrived.shape[1] - 8
    core = place[0]

    def half(side):
        return jnp.sum(arrived[pl.ds(side * tp, tp), :rank].astype(F32), axis=0)

    return half(core), half(1 - core)


def power_kernel(place, arrived, near, far, out):
    cols = near.shape[2] * 2 // 5
    own, other = left_sum(place, arrived)
    near_matrix, far_matrix = matrix_of(near, cols), matrix_of(far, cols)
    right = times_exact(own, near_matrix, ((1,), (0,))) + times_exact(other, far_matrix, ((1,), (0,)))
    half = own.shape[1]
    for side, matrix in enumerate((near_matrix, far_matrix)):
        left = times_exact(right, matrix, ((1,), (1,))).astype(BF16)
        out[:, :, side * half : (side + 1) * half] = jnp.broadcast_to(left, (out.shape[0], *left.shape))


def factor_kernel(place, arrived, after, out, vector):
    del after
    peers, filled = arrived.shape[:2]
    tp, rank = peers // 2, filled - 8
    count = vector.shape[0] // tp
    for peer in range(peers):
        side, column = peer // tp, peer % tp
        tile = arrived[peer, rank:, :LANES].astype(F32)
        for row in range(3 if side == 0 else count - 3):
            vector[column * count + 3 * side + row] = tile[row : row + 1] + tile[row + 3 : row + 4]
    own, other = left_sum(place, arrived)
    out[...] = gram_inverse(jnp.concatenate([own, other], 1))


def finish_kernel(
    place,
    parts,
    inverse_one,
    near,
    far,
    gradients,
    feedback,
    momentum,
    master,
    new_feedback,
    weight,
    new_momentum,
    new_master,
    ortho_terms,
    right_terms,
    feedback_buffer,
    weight_buffer,
    base,
    owned,
    sems,
    *,
    replicas,
):
    core, chip = place[0], place[1]
    chips, pair, cols = feedback.shape
    rows = pair // 2
    half = chips * rows
    for side, ref in ((core, near), (1 - core, far)):
        base[side] = ref[:, :, cols + LANES :]
    left = product(inverse_one[...], jnp.sum(parts[...].astype(F32), axis=0), ((1,), (0,)), PRECISE)
    ortho = product(gram_inverse(left), left, ((1,), (0,)), PRECISE)
    right = times_exact(ortho[:, :half], matrix_of(near, cols), ((1,), (0,)))
    right += times_exact(ortho[:, half:], matrix_of(far, cols), ((1,), (0,)))
    right_high, right_low = split(right / replicas)
    right_terms[...] = jnp.concatenate([right_high, right_low, right_high], 0)
    for side, start in enumerate((core * half, (1 - core) * half)):
        high, low = split(ortho[:, side * half : (side + 1) * half])
        ortho_terms[:, pl.ds(pl.multiple_of(start, LANES), half)] = jnp.concatenate([high, high, low], 0)
    step = chips // CHUNKS
    copies = []
    for chunk in range(CHUNKS):
        span = slice(chunk * step, (chunk + 1) * step)
        sides = []
        for side in range(2):
            at = side * half + chunk * step * rows
            terms = ortho_terms[:, at : at + step * rows]
            sides.append(product(terms, right_terms[...], ((0,), (0,))).reshape(step, rows, cols))
        approx = jnp.concatenate(sides, 1)
        owned[:, span] = jnp.stack(sides, 0)
        feedback_buffer[span] = gradients[span].astype(F32) + feedback[span] - approx
        kept = [base[side, span].astype(F32) for side in range(2)]
        weight_buffer[span] = (jnp.concatenate(kept, 1) - LEARN_RATE * approx).astype(BF16)
        for which, (source, target) in enumerate(((feedback_buffer, new_feedback), (weight_buffer, weight))):
            copy = pltpu.make_async_copy(source.at[span], target.at[span], sems.at[chunk, which])
            copy.start()
            copies.append(copy)
    moved = MOMENTUM_RATE * momentum[...] + owned[core, chip]
    new_momentum[...] = moved
    new_master[...] = master[...] - LEARN_RATE * moved
    for copy in copies:
        copy.wait()


def shards(
    gradients,
    feedback,
    warm_factor,
    momentum,
    master_owned,
    vector_grads,
    vector_params,
    vector_momentum,
):
    replicas = lax.axis_size(REP)
    chips = lax.axis_size(CHIPS)
    tp = lax.axis_size("tp")
    core = lax.axis_index("c")
    rows, cols = gradients.shape[1:]
    owned = momentum.shape[0]
    rank = warm_factor.shape[1]
    half = rows // 2
    place = jnp.stack([core, lax.axis_index(CHIPS), lax.axis_index("tp")]).astype(jnp.int32)
    by_pair = (chips, 2 * owned, cols)
    by_owner = (chips, 2, owned, cols)
    lines = vector_grads.reshape(-1, 1, LANES)
    halves = (gradients.reshape(by_owner), feedback.reshape(by_owner))
    buffers = [
        pltpu.VMEM((chips, owned, cols), BF16),
        pltpu.VMEM((chips, owned, cols), F32),
        pltpu.SemaphoreType.DMA((CHUNKS, 2)),
    ]

    sent = pl.pallas_call(
        send_kernel,
        out_shape=jax.ShapeDtypeStruct((chips + 1, owned, cols), BF16),
        in_specs=[SMEM, ANY, ANY, VMEM],
        out_specs=VMEM,
        scratch_shapes=buffers,
        name="send",
    )(place, *halves, lines)
    received = lax.ppermute(sent, "c", SWAP)
    kept = pl.pallas_call(
        keep_kernel,
        out_shape=jax.ShapeDtypeStruct((chips, owned, cols), F32),
        in_specs=[SMEM, ANY, ANY, ANY],
        out_specs=VMEM,
        scratch_shapes=buffers,
        name="keep",
    )(place, *halves, sent)
    paired = pl.pallas_call(
        pair_kernel,
        out_shape=jax.ShapeDtypeStruct((chips, owned, cols), BF16),
        in_specs=[VMEM] * 2,
        out_specs=VMEM,
        compiler_params=SMALL,
        name="pair",
    )(kept, received)
    arrived = exchange(paired, CHIPS)

    shared_cols = 2 * cols + LANES
    shared = pl.pallas_call(
        share_kernel,
        out_shape=jax.ShapeDtypeStruct((chips, owned, shared_cols), BF16),
        in_specs=[SMEM] + [VMEM] * 5,
        out_specs=VMEM,
        compiler_params=SMALL,
        name="share",
    )(place, arrived, received, lines, momentum, master_owned)
    near = exchange(shared, CHIPS)
    far = lax.ppermute(near, "c", SWAP)
    left = pl.pallas_call(
        left_kernel,
        out_shape=jax.ShapeDtypeStruct((2 * tp, rank + 8, half), BF16),
        in_specs=[VMEM] * 2,
        out_specs=VMEM,
        compiler_params=SMALL,
        name="left",
    )(near, warm_factor)
    left = exchange(left, ("c", "tp"))
    parts = pl.pallas_call(
        power_kernel,
        out_shape=jax.ShapeDtypeStruct((tp, rank, rows), BF16),
        in_specs=[SMEM] + [VMEM] * 3,
        out_specs=VMEM,
        compiler_params=SMALL,
        name="power",
    )(place, left, near, far)
    inverse_one, vector = pl.pallas_call(
        factor_kernel,
        out_shape=(jax.ShapeDtypeStruct((rank, rank), F32), jax.ShapeDtypeStruct(lines.shape, F32)),
        in_specs=[SMEM, VMEM, ANY],
        out_specs=(VMEM, VMEM),
        compiler_params=SMALL,
        name="factor",
    )(place, left, parts)
    parts = exchange(parts, "tp")
    vector_sum = vector.reshape(-1)

    new_feedback, weight, new_momentum, new_master = pl.pallas_call(
        functools.partial(finish_kernel, replicas=replicas),
        out_shape=(
            jax.ShapeDtypeStruct(by_pair, F32),
            jax.ShapeDtypeStruct(by_pair, BF16),
            jax.ShapeDtypeStruct(momentum.shape, F32),
            jax.ShapeDtypeStruct(momentum.shape, F32),
        ),
        in_specs=[SMEM] + [VMEM] * 8,
        out_specs=(ANY, ANY, VMEM, VMEM),
        scratch_shapes=[
            pltpu.VMEM((3 * rank, rows), BF16),
            pltpu.VMEM((3 * rank, cols), BF16),
            pltpu.VMEM(by_pair, F32),
            pltpu.VMEM(by_pair, BF16),
            pltpu.VMEM((2, chips, owned, cols), BF16),
            pltpu.VMEM((2, chips, owned, cols), F32),
            pltpu.SemaphoreType.DMA((CHUNKS, 2)),
        ],
        compiler_params=LARGE,
        name="finish",
    )(
        place,
        parts,
        inverse_one,
        near,
        far,
        gradients.reshape(by_pair),
        feedback.reshape(by_pair),
        momentum,
        master_owned,
    )
    new_vector_momentum = MOMENTUM_RATE * vector_momentum + vector_sum / replicas
    new_vector_params = vector_params - LEARN_RATE * new_vector_momentum
    return (
        new_feedback.reshape(feedback.shape),
        new_momentum,
        new_master,
        weight.reshape(rows, cols),
        new_vector_params,
        new_vector_momentum,
    )


def solution(mesh):
    finer = Mesh(mesh.devices.reshape(8, 8, 2, mesh.shape["tp"]), ("y", "z", "c", "tp"))
    in_specs = (
        P(REP, None, "tp"),
        P(REP, None, "tp"),
        P("tp", None),
        P(REP, "tp"),
        P(REP, "tp"),
        P(REP, None),
        P(),
        P(),
    )
    out_specs = (P(REP, None, "tp"), P(REP, "tp"), P(REP, "tp"), P(None, "tp"), P(), P())
    return jax.shard_map(
        shards, mesh=finer, in_specs=in_specs, out_specs=out_specs, check_vma=False
    )
```

```python
import functools

import jax
import jax.numpy as jnp
from jax import lax
from jax.experimental import pallas as pl
from jax.experimental.pallas import tpu as pltpu
from jax.sharding import Mesh
from jax.sharding import PartitionSpec as P

REP = ("y", "z", "c")
CHIPS = ("y", "z")
PRECISE = lax.Precision.HIGHEST
MOMENTUM_RATE = 0.9
LEARN_RATE = 0.5
F32 = jnp.float32
BF16 = jnp.bfloat16
SWAP = ((0, 1), (1, 0))
LANES = 128
PIVOTS = 8
CHUNKS = 4
TP = 4
VMEM = pl.BlockSpec(memory_space=pltpu.VMEM)
ANY = pl.BlockSpec(memory_space=pl.ANY)
SMALL = pltpu.CompilerParams(vmem_limit_bytes=8 << 20)
LARGE = pltpu.CompilerParams(vmem_limit_bytes=20 << 20)


def split(values):
    high = values.astype(BF16)
    return high, (values - high.astype(F32)).astype(BF16)


def exchange(array, axis):
    return lax.all_to_all(array, axis, 0, 0, tiled=True)


def product(left, right, dims, precision=None):
    return lax.dot_general(left, right, (dims, ((), ())), precision=precision, preferred_element_type=F32)


def times_exact(factor, exact, dims):
    both = product(jnp.concatenate(split(factor), 0), exact, dims)
    rows = factor.shape[0]
    return both[:rows] + both[rows:]


def lower_inverse(gram):
    n = gram.shape[0]
    lane = lax.broadcasted_iota(jnp.int32, (n, LANES), 1)
    row = lax.broadcasted_iota(jnp.int32, (n, LANES), 0)
    eye = jnp.where(lane == row + n, 1.0, 0.0).astype(F32)
    work = jnp.concatenate([gram, jnp.zeros((n, LANES - n), F32)], 1) + eye
    inverses = []
    for first in range(0, n, PIVOTS):
        cols = [jnp.broadcast_to(work[:, first + j : first + j + 1], (n, LANES)) for j in range(PIVOTS)]
        lines = [work[first + j : first + j + 1, :] for j in range(PIVOTS)]
        for j in range(PIVOTS):
            at = first + j
            inverse = 1.0 / cols[j][at : at + 1, :]
            inverses.append(inverse)
            scaled = lines[j] * inverse
            below = jnp.where(row > at, cols[j], 0.0)
            for m in range(j + 1, PIVOTS):
                lines[m] = lines[m] - cols[j][first + m : first + m + 1, :] * scaled
                cols[m] = cols[m] - below * (cols[m][at : at + 1, :] * inverse)
            work = work - below * scaled
    return (work * jnp.sqrt(jnp.concatenate(inverses, 0)))[:, n : 2 * n]


def gram_inverse(left):
    return lower_inverse(product(left, left, ((1,), (1,)), PRECISE))


def quarter_of(vector):
    count = vector.shape[0] // TP
    rows = [vector[lax.axis_index("tp") * count + j] for j in range(count)]
    return jnp.concatenate(rows + [jnp.zeros((8 - count, LANES), F32)], 0)


def send_kernel(gradients, feedback, vector, out):
    side = 1 - lax.axis_index("c")
    chips = gradients.shape[0]
    out[:chips] = (gradients[:, side].astype(F32) + feedback[:, side]).astype(BF16)
    out[chips] = jnp.concatenate(split(quarter_of(vector)), 1)


def keep_kernel(gradients, feedback, after, out):
    del after
    side = lax.axis_index("c")
    out[...] = gradients[:, side].astype(F32) + feedback[:, side]


def pair_kernel(kept, received, out):
    out[...] = (kept[...] + received[: kept.shape[0]].astype(F32)).astype(BF16)


def packed_rows(rows):
    high, low = split(rows)
    return jnp.concatenate([high.astype(F32), low.astype(F32), jnp.zeros((2, LANES), F32)], 0)


def share_kernel(arrived, received, vector, momentum, master, out):
    total = jnp.sum(arrived[...].astype(F32), axis=0)
    other = received[received.shape[0] - 1].astype(F32)
    quarter = quarter_of(vector) + other[:, :LANES] + other[:, LANES:]
    rows = jnp.where(lax.axis_index("c") == 0, quarter[0:3], quarter[3:6])
    base = master[...] - LEARN_RATE * MOMENTUM_RATE * momentum[...]
    shared = jnp.concatenate([total, packed_rows(rows), base], 1).astype(BF16)
    out[...] = jnp.broadcast_to(shared, out.shape)


def matrix_of(ref, cols):
    return ref[:, :, :cols].reshape(-1, cols)


def left_kernel(near, factor, out):
    cols = factor.shape[1]
    left = times_exact(factor[...], matrix_of(near, cols), ((1,), (1,)))
    spread = jnp.sum(near[:, :, cols : cols + LANES].astype(F32), axis=0)
    rows = packed_rows(spread[0:3] + spread[3:6])
    rows = jnp.concatenate([rows, jnp.zeros((8, left.shape[1] - LANES), F32)], 1)
    both = jnp.concatenate([left, rows], 0).astype(BF16)
    out[...] = jnp.broadcast_to(both, out.shape)


def left_sum(arrived):
    tp = arrived.shape[0] // 2
    rank = arrived.shape[1] - 8
    core = lax.axis_index("c")

    def half(side):
        return jnp.sum(arrived[pl.ds(side * tp, tp), :rank].astype(F32), axis=0)

    return half(core), half(1 - core)


def power_kernel(arrived, near, far, out):
    cols = near.shape[2] * 2 // 5
    own, other = left_sum(arrived)
    near_matrix, far_matrix = matrix_of(near, cols), matrix_of(far, cols)
    right = times_exact(own, near_matrix, ((1,), (0,))) + times_exact(other, far_matrix, ((1,), (0,)))
    half = own.shape[1]
    for side, matrix in enumerate((near_matrix, far_matrix)):
        left = times_exact(right, matrix, ((1,), (1,))).astype(BF16)
        out[:, :, side * half : (side + 1) * half] = jnp.broadcast_to(left, (out.shape[0], *left.shape))


def factor_kernel(arrived, after, out, vector):
    del after
    peers, filled = arrived.shape[:2]
    tp, rank = peers // 2, filled - 8
    count = vector.shape[0] // tp
    for peer in range(peers):
        side, column = peer // tp, peer % tp
        tile = arrived[peer, rank:, :LANES].astype(F32)
        for row in range(3 if side == 0 else count - 3):
            vector[column * count + 3 * side + row] = tile[row : row + 1] + tile[row + 3 : row + 4]
    own, other = left_sum(arrived)
    out[...] = gram_inverse(jnp.concatenate([own, other], 1))


def finish_kernel(
    parts,
    inverse_one,
    near,
    far,
    gradients,
    feedback,
    momentum,
    master,
    new_feedback,
    weight,
    new_momentum,
    new_master,
    ortho_terms,
    right_terms,
    feedback_buffer,
    weight_buffer,
    base,
    owned,
    sems,
    *,
    replicas,
):
    core, chip = lax.axis_index("c"), lax.axis_index(CHIPS)
    chips, pair, cols = feedback.shape
    rows = pair // 2
    half = chips * rows
    for side, ref in ((core, near), (1 - core, far)):
        base[side] = ref[:, :, cols + LANES :]
    left = product(inverse_one[...], jnp.sum(parts[...].astype(F32), axis=0), ((1,), (0,)), PRECISE)
    ortho = product(gram_inverse(left), left, ((1,), (0,)), PRECISE)
    right = times_exact(ortho[:, :half], matrix_of(near, cols), ((1,), (0,)))
    right += times_exact(ortho[:, half:], matrix_of(far, cols), ((1,), (0,)))
    right_high, right_low = split(right / replicas)
    right_terms[...] = jnp.concatenate([right_high, right_low, right_high], 0)
    for side, start in enumerate((core * half, (1 - core) * half)):
        high, low = split(ortho[:, side * half : (side + 1) * half])
        ortho_terms[:, pl.ds(pl.multiple_of(start, LANES), half)] = jnp.concatenate([high, high, low], 0)
    step = chips // CHUNKS
    copies = []
    for chunk in range(CHUNKS):
        span = slice(chunk * step, (chunk + 1) * step)
        sides = []
        for side in range(2):
            at = side * half + chunk * step * rows
            terms = ortho_terms[:, at : at + step * rows]
            sides.append(product(terms, right_terms[...], ((0,), (0,))).reshape(step, rows, cols))
        approx = jnp.concatenate(sides, 1)
        owned[:, span] = jnp.stack(sides, 0)
        feedback_buffer[span] = gradients[span].astype(F32) + feedback[span] - approx
        kept = [base[side, span].astype(F32) for side in range(2)]
        weight_buffer[span] = (jnp.concatenate(kept, 1) - LEARN_RATE * approx).astype(BF16)
        for which, (source, target) in enumerate(((feedback_buffer, new_feedback), (weight_buffer, weight))):
            copy = pltpu.make_async_copy(source.at[span], target.at[span], sems.at[chunk, which])
            copy.start()
            copies.append(copy)
    moved = MOMENTUM_RATE * momentum[...] + owned[core, chip]
    new_momentum[...] = moved
    new_master[...] = master[...] - LEARN_RATE * moved
    for copy in copies:
        copy.wait()


def shards(
    gradients,
    feedback,
    warm_factor,
    momentum,
    master_owned,
    vector_grads,
    vector_params,
    vector_momentum,
):
    replicas = lax.axis_size(REP)
    chips = lax.axis_size(CHIPS)
    tp = lax.axis_size("tp")
    rows, cols = gradients.shape[1:]
    owned = momentum.shape[0]
    rank = warm_factor.shape[1]
    half = rows // 2
    by_pair = (chips, 2 * owned, cols)
    by_owner = (chips, 2, owned, cols)
    lines = vector_grads.reshape(-1, 1, LANES)
    halves = (gradients.reshape(by_owner), feedback.reshape(by_owner))
    sent = pl.pallas_call(
        send_kernel,
        out_shape=jax.ShapeDtypeStruct((chips + 1, owned, cols), BF16),
        in_specs=[VMEM] * 3,
        out_specs=VMEM,
        compiler_params=SMALL,
        name="send",
    )(*halves, lines)
    received = lax.ppermute(sent, "c", SWAP)
    kept = pl.pallas_call(
        keep_kernel,
        out_shape=jax.ShapeDtypeStruct((chips, owned, cols), F32),
        in_specs=[VMEM, VMEM, ANY],
        out_specs=VMEM,
        compiler_params=SMALL,
        name="keep",
    )(*halves, sent)
    paired = pl.pallas_call(
        pair_kernel,
        out_shape=jax.ShapeDtypeStruct((chips, owned, cols), BF16),
        in_specs=[VMEM] * 2,
        out_specs=VMEM,
        compiler_params=SMALL,
        name="pair",
    )(kept, received)
    arrived = exchange(paired, CHIPS)

    shared_cols = 2 * cols + LANES
    shared = pl.pallas_call(
        share_kernel,
        out_shape=jax.ShapeDtypeStruct((chips, owned, shared_cols), BF16),
        in_specs=[VMEM] * 5,
        out_specs=VMEM,
        compiler_params=SMALL,
        name="share",
    )(arrived, received, lines, momentum, master_owned)
    near = exchange(shared, CHIPS)
    far = lax.ppermute(near, "c", SWAP)
    left = pl.pallas_call(
        left_kernel,
        out_shape=jax.ShapeDtypeStruct((2 * tp, rank + 8, half), BF16),
        in_specs=[VMEM] * 2,
        out_specs=VMEM,
        compiler_params=SMALL,
        name="left",
    )(near, warm_factor.T)
    left = exchange(left, ("c", "tp"))
    parts = pl.pallas_call(
        power_kernel,
        out_shape=jax.ShapeDtypeStruct((tp, rank, rows), BF16),
        in_specs=[VMEM] * 3,
        out_specs=VMEM,
        compiler_params=SMALL,
        name="power",
    )(left, near, far)
    inverse_one, vector = pl.pallas_call(
        factor_kernel,
        out_shape=(jax.ShapeDtypeStruct((rank, rank), F32), jax.ShapeDtypeStruct(lines.shape, F32)),
        in_specs=[VMEM, ANY],
        out_specs=(VMEM, VMEM),
        compiler_params=SMALL,
        name="factor",
    )(left, parts)
    parts = exchange(parts, "tp")
    vector_sum = vector.reshape(-1)

    new_feedback, weight, new_momentum, new_master = pl.pallas_call(
        functools.partial(finish_kernel, replicas=replicas),
        out_shape=(
            jax.ShapeDtypeStruct(by_pair, F32),
            jax.ShapeDtypeStruct(by_pair, BF16),
            jax.ShapeDtypeStruct(momentum.shape, F32),
            jax.ShapeDtypeStruct(momentum.shape, F32),
        ),
        in_specs=[VMEM] * 8,
        out_specs=(ANY, ANY, VMEM, VMEM),
        scratch_shapes=[
            pltpu.VMEM((3 * rank, rows), BF16),
            pltpu.VMEM((3 * rank, cols), BF16),
            pltpu.VMEM(by_pair, F32),
            pltpu.VMEM(by_pair, BF16),
            pltpu.VMEM((2, chips, owned, cols), BF16),
            pltpu.VMEM((2, chips, owned, cols), F32),
            pltpu.SemaphoreType.DMA((CHUNKS, 2)),
        ],
        compiler_params=LARGE,
        name="finish",
    )(
        parts,
        inverse_one,
        near,
        far,
        gradients.reshape(by_pair),
        feedback.reshape(by_pair),
        momentum,
        master_owned,
    )
    new_vector_momentum = MOMENTUM_RATE * vector_momentum + vector_sum / replicas
    new_vector_params = vector_params - LEARN_RATE * new_vector_momentum
    return (
        new_feedback.reshape(feedback.shape),
        new_momentum,
        new_master,
        weight.reshape(rows, cols),
        new_vector_params,
        new_vector_momentum,
    )


def solution(mesh):
    finer = Mesh(mesh.devices.reshape(8, 8, 2, mesh.shape["tp"]), ("y", "z", "c", "tp"))
    in_specs = (
        P(REP, None, "tp"),
        P(REP, None, "tp"),
        P("tp", None),
        P(REP, "tp"),
        P(REP, "tp"),
        P(REP, None),
        P(),
        P(),
    )
    out_specs = (P(REP, None, "tp"), P(REP, "tp"), P(REP, "tp"), P(None, "tp"), P(), P())
    return jax.shard_map(
        shards, mesh=finer, in_specs=in_specs, out_specs=out_specs, check_vma=False
    )
```

```python
import functools

import jax
import jax.numpy as jnp
from jax import lax
from jax.experimental import pallas as pl
from jax.experimental.pallas import tpu as pltpu
from jax.sharding import Mesh
from jax.sharding import PartitionSpec as P

REP = ("y", "z", "c")
CHIPS = ("y", "z")
PRECISE = lax.Precision.HIGHEST
MOMENTUM_RATE = 0.9
LEARN_RATE = 0.5
F32 = jnp.float32
BF16 = jnp.bfloat16
SWAP = ((0, 1), (1, 0))
LANES = 128
PIVOTS = 8
CHUNKS = 4
TP = 4
VMEM = pl.BlockSpec(memory_space=pltpu.VMEM)
ANY = pl.BlockSpec(memory_space=pl.ANY)
SMALL = pltpu.CompilerParams(vmem_limit_bytes=8 << 20)
PACK = pltpu.CompilerParams(vmem_limit_bytes=54400 << 10)
LARGE = pltpu.CompilerParams(vmem_limit_bytes=20 << 20)


def split(values):
    high = values.astype(BF16)
    return high, (values - high.astype(F32)).astype(BF16)


def exchange(array, axis):
    return lax.all_to_all(array, axis, 0, 0, tiled=True)


def product(left, right, dims, precision=None):
    return lax.dot_general(left, right, (dims, ((), ())), precision=precision, preferred_element_type=F32)


def times_exact(factor, exact, dims):
    both = product(jnp.concatenate(split(factor), 0), exact, dims)
    rows = factor.shape[0]
    return both[:rows] + both[rows:]


def lower_inverse(gram):
    n = gram.shape[0]
    lane = lax.broadcasted_iota(jnp.int32, (n, LANES), 1)
    row = lax.broadcasted_iota(jnp.int32, (n, LANES), 0)
    eye = jnp.where(lane == row + n, 1.0, 0.0).astype(F32)
    work = jnp.concatenate([gram, jnp.zeros((n, LANES - n), F32)], 1) + eye
    inverses = []
    for first in range(0, n, PIVOTS):
        cols = [jnp.broadcast_to(work[:, first + j : first + j + 1], (n, LANES)) for j in range(PIVOTS)]
        lines = [work[first + j : first + j + 1, :] for j in range(PIVOTS)]
        for j in range(PIVOTS):
            at = first + j
            inverse = 1.0 / cols[j][at : at + 1, :]
            inverses.append(inverse)
            scaled = lines[j] * inverse
            below = jnp.where(row > at, cols[j], 0.0)
            for m in range(j + 1, PIVOTS):
                lines[m] = lines[m] - cols[j][first + m : first + m + 1, :] * scaled
                cols[m] = cols[m] - below * (cols[m][at : at + 1, :] * inverse)
            work = work - below * scaled
    return (work * jnp.sqrt(jnp.concatenate(inverses, 0)))[:, n : 2 * n]


def gram_inverse(left):
    return lower_inverse(product(left, left, ((1,), (1,)), PRECISE))


def quarter_of(vector):
    count = vector.shape[0] // TP
    rows = [vector[lax.axis_index("tp") * count + j] for j in range(count)]
    return jnp.concatenate(rows + [jnp.zeros((8 - count, LANES), F32)], 0)


def pack_kernel(gradients, feedback, vector, sent, kept, narrow, wide, line, sems):
    core = lax.axis_index("c")
    chips = gradients.shape[0]
    step = chips // CHUNKS
    spans = [slice(chunk * step, (chunk + 1) * step) for chunk in range(CHUNKS)]
    last = pltpu.make_async_copy(vector, line, sems.at[CHUNKS, 0])
    copies = []
    for chunk, span in enumerate(spans):
        pair = ((gradients, narrow), (feedback, wide))
        copies += [pltpu.make_async_copy(s.at[span], t.at[span], sems.at[chunk, w]) for w, (s, t) in enumerate(pair)]
    for copy in (*copies, last):
        copy.start()
    for chunk, span in enumerate(spans):
        copies[2 * chunk].wait()
        copies[2 * chunk + 1].wait()
        sent[span] = (narrow[span, 1 - core].astype(F32) + wide[span, 1 - core]).astype(BF16)
        kept[span] = narrow[span, core].astype(F32) + wide[span, core]
    last.wait()
    sent[chips] = jnp.concatenate(split(quarter_of(line)), 1)


def pair_kernel(kept, received, out):
    out[...] = (kept[...] + received[: kept.shape[0]].astype(F32)).astype(BF16)


def packed_rows(rows):
    high, low = split(rows)
    return jnp.concatenate([high.astype(F32), low.astype(F32), jnp.zeros((2, LANES), F32)], 0)


def share_kernel(arrived, received, vector, momentum, master, out):
    total = jnp.sum(arrived[...].astype(F32), axis=0)
    other = received[received.shape[0] - 1].astype(F32)
    quarter = quarter_of(vector) + other[:, :LANES] + other[:, LANES:]
    rows = jnp.where(lax.axis_index("c") == 0, quarter[0:3], quarter[3:6])
    base = master[...] - LEARN_RATE * MOMENTUM_RATE * momentum[...]
    shared = jnp.concatenate([total, packed_rows(rows), base], 1).astype(BF16)
    out[...] = jnp.broadcast_to(shared, out.shape)


def matrix_of(ref, cols):
    return ref[:, :, :cols].reshape(-1, cols)


def left_kernel(near, factor, out):
    cols = factor.shape[1]
    left = times_exact(factor[...], matrix_of(near, cols), ((1,), (1,)))
    spread = jnp.sum(near[:, :, cols : cols + LANES].astype(F32), axis=0)
    rows = packed_rows(spread[0:3] + spread[3:6])
    rows = jnp.concatenate([rows, jnp.zeros((8, left.shape[1] - LANES), F32)], 1)
    both = jnp.concatenate([left, rows], 0).astype(BF16)
    out[...] = jnp.broadcast_to(both, out.shape)


def left_sum(arrived):
    tp = arrived.shape[0] // 2
    rank = arrived.shape[1] - 8
    core = lax.axis_index("c")

    def half(side):
        return jnp.sum(arrived[pl.ds(side * tp, tp), :rank].astype(F32), axis=0)

    return half(core), half(1 - core)


def power_kernel(arrived, near, far, out):
    cols = near.shape[2] * 2 // 5
    own, other = left_sum(arrived)
    near_matrix, far_matrix = matrix_of(near, cols), matrix_of(far, cols)
    right = times_exact(own, near_matrix, ((1,), (0,))) + times_exact(other, far_matrix, ((1,), (0,)))
    half = own.shape[1]
    for side, matrix in enumerate((near_matrix, far_matrix)):
        left = times_exact(right, matrix, ((1,), (1,))).astype(BF16)
        out[:, :, side * half : (side + 1) * half] = jnp.broadcast_to(left, (out.shape[0], *left.shape))


def factor_kernel(arrived, after, out, vector):
    del after
    peers, filled = arrived.shape[:2]
    tp, rank = peers // 2, filled - 8
    count = vector.shape[0] // tp
    for peer in range(peers):
        side, column = peer // tp, peer % tp
        tile = arrived[peer, rank:, :LANES].astype(F32)
        for row in range(3 if side == 0 else count - 3):
            vector[column * count + 3 * side + row] = tile[row : row + 1] + tile[row + 3 : row + 4]
    own, other = left_sum(arrived)
    out[...] = gram_inverse(jnp.concatenate([own, other], 1))


def finish_kernel(
    parts,
    inverse_one,
    near,
    far,
    gradients,
    feedback,
    momentum,
    master,
    new_feedback,
    weight,
    new_momentum,
    new_master,
    ortho_terms,
    right_terms,
    feedback_buffer,
    weight_buffer,
    base,
    owned,
    sems,
    *,
    replicas,
):
    core, chip = lax.axis_index("c"), lax.axis_index(CHIPS)
    chips, pair, cols = feedback.shape
    rows = pair // 2
    half = chips * rows
    for side, ref in ((core, near), (1 - core, far)):
        base[side] = ref[:, :, cols + LANES :]
    left = product(inverse_one[...], jnp.sum(parts[...].astype(F32), axis=0), ((1,), (0,)), PRECISE)
    ortho = product(gram_inverse(left), left, ((1,), (0,)), PRECISE)
    right = times_exact(ortho[:, :half], matrix_of(near, cols), ((1,), (0,)))
    right += times_exact(ortho[:, half:], matrix_of(far, cols), ((1,), (0,)))
    right_high, right_low = split(right / replicas)
    right_terms[...] = jnp.concatenate([right_high, right_low, right_high], 0)
    for side, start in enumerate((core * half, (1 - core) * half)):
        high, low = split(ortho[:, side * half : (side + 1) * half])
        ortho_terms[:, pl.ds(pl.multiple_of(start, LANES), half)] = jnp.concatenate([high, high, low], 0)
    step = chips // CHUNKS
    copies = []
    for chunk in range(CHUNKS):
        span = slice(chunk * step, (chunk + 1) * step)
        sides = []
        for side in range(2):
            at = side * half + chunk * step * rows
            terms = ortho_terms[:, at : at + step * rows]
            sides.append(product(terms, right_terms[...], ((0,), (0,))).reshape(step, rows, cols))
        approx = jnp.concatenate(sides, 1)
        owned[:, span] = jnp.stack(sides, 0)
        feedback_buffer[span] = gradients[span].astype(F32) + feedback[span] - approx
        kept = [base[side, span].astype(F32) for side in range(2)]
        weight_buffer[span] = (jnp.concatenate(kept, 1) - LEARN_RATE * approx).astype(BF16)
        for which, (source, target) in enumerate(((feedback_buffer, new_feedback), (weight_buffer, weight))):
            copy = pltpu.make_async_copy(source.at[span], target.at[span], sems.at[chunk, which])
            copy.start()
            copies.append(copy)
    moved = MOMENTUM_RATE * momentum[...] + owned[core, chip]
    new_momentum[...] = moved
    new_master[...] = master[...] - LEARN_RATE * moved
    for copy in copies:
        copy.wait()


def shards(
    gradients,
    feedback,
    warm_factor,
    momentum,
    master_owned,
    vector_grads,
    vector_params,
    vector_momentum,
):
    replicas = lax.axis_size(REP)
    chips = lax.axis_size(CHIPS)
    tp = lax.axis_size("tp")
    rows, cols = gradients.shape[1:]
    owned = momentum.shape[0]
    rank = warm_factor.shape[1]
    half = rows // 2
    by_pair = (chips, 2 * owned, cols)
    by_owner = (chips, 2, owned, cols)
    lines = vector_grads.reshape(-1, 1, LANES)
    halves = (gradients.reshape(by_owner), feedback.reshape(by_owner))
    sent, kept = pl.pallas_call(
        pack_kernel,
        out_shape=(
            jax.ShapeDtypeStruct((chips + 1, owned, cols), BF16),
            jax.ShapeDtypeStruct((chips, owned, cols), F32),
        ),
        in_specs=[ANY] * 3,
        out_specs=(VMEM, VMEM),
        scratch_shapes=[
            pltpu.VMEM(by_owner, BF16),
            pltpu.VMEM(by_owner, F32),
            pltpu.VMEM(lines.shape, F32),
            pltpu.SemaphoreType.DMA((CHUNKS + 1, 2)),
        ],
        compiler_params=PACK,
        name="pack",
    )(*halves, lines)
    received = lax.ppermute(sent, "c", SWAP)
    paired = pl.pallas_call(
        pair_kernel,
        out_shape=jax.ShapeDtypeStruct((chips, owned, cols), BF16),
        in_specs=[VMEM] * 2,
        out_specs=VMEM,
        compiler_params=SMALL,
        name="pair",
    )(kept, received)
    arrived = exchange(paired, CHIPS)

    shared_cols = 2 * cols + LANES
    shared = pl.pallas_call(
        share_kernel,
        out_shape=jax.ShapeDtypeStruct((chips, owned, shared_cols), BF16),
        in_specs=[VMEM] * 5,
        out_specs=VMEM,
        compiler_params=SMALL,
        name="share",
    )(arrived, received, lines, momentum, master_owned)
    near = exchange(shared, CHIPS)
    far = lax.ppermute(near, "c", SWAP)
    left = pl.pallas_call(
        left_kernel,
        out_shape=jax.ShapeDtypeStruct((2 * tp, rank + 8, half), BF16),
        in_specs=[VMEM] * 2,
        out_specs=VMEM,
        compiler_params=SMALL,
        name="left",
    )(near, warm_factor.T)
    left = exchange(left, ("c", "tp"))
    parts = pl.pallas_call(
        power_kernel,
        out_shape=jax.ShapeDtypeStruct((tp, rank, rows), BF16),
        in_specs=[VMEM] * 3,
        out_specs=VMEM,
        compiler_params=SMALL,
        name="power",
    )(left, near, far)
    inverse_one, vector = pl.pallas_call(
        factor_kernel,
        out_shape=(jax.ShapeDtypeStruct((rank, rank), F32), jax.ShapeDtypeStruct(lines.shape, F32)),
        in_specs=[VMEM, ANY],
        out_specs=(VMEM, VMEM),
        compiler_params=SMALL,
        name="factor",
    )(left, parts)
    parts = exchange(parts, "tp")
    vector_sum = vector.reshape(-1)

    new_feedback, weight, new_momentum, new_master = pl.pallas_call(
        functools.partial(finish_kernel, replicas=replicas),
        out_shape=(
            jax.ShapeDtypeStruct(by_pair, F32),
            jax.ShapeDtypeStruct(by_pair, BF16),
            jax.ShapeDtypeStruct(momentum.shape, F32),
            jax.ShapeDtypeStruct(momentum.shape, F32),
        ),
        in_specs=[VMEM] * 8,
        out_specs=(ANY, ANY, VMEM, VMEM),
        scratch_shapes=[
            pltpu.VMEM((3 * rank, rows), BF16),
            pltpu.VMEM((3 * rank, cols), BF16),
            pltpu.VMEM(by_pair, F32),
            pltpu.VMEM(by_pair, BF16),
            pltpu.VMEM((2, chips, owned, cols), BF16),
            pltpu.VMEM((2, chips, owned, cols), F32),
            pltpu.SemaphoreType.DMA((CHUNKS, 2)),
        ],
        compiler_params=LARGE,
        name="finish",
    )(
        parts,
        inverse_one,
        near,
        far,
        gradients.reshape(by_pair),
        feedback.reshape(by_pair),
        momentum,
        master_owned,
    )
    new_vector_momentum = MOMENTUM_RATE * vector_momentum + vector_sum / replicas
    new_vector_params = vector_params - LEARN_RATE * new_vector_momentum
    return (
        new_feedback.reshape(feedback.shape),
        new_momentum,
        new_master,
        weight.reshape(rows, cols),
        new_vector_params,
        new_vector_momentum,
    )


def solution(mesh):
    finer = Mesh(mesh.devices.reshape(8, 8, 2, mesh.shape["tp"]), ("y", "z", "c", "tp"))
    in_specs = (
        P(REP, None, "tp"),
        P(REP, None, "tp"),
        P("tp", None),
        P(REP, "tp"),
        P(REP, "tp"),
        P(REP, None),
        P(),
        P(),
    )
    out_specs = (P(REP, None, "tp"), P(REP, "tp"), P(REP, "tp"), P(None, "tp"), P(), P())
    return jax.shard_map(
        shards, mesh=finer, in_specs=in_specs, out_specs=out_specs, check_vma=False
    )
```

```python
import functools

import jax
import jax.numpy as jnp
from jax import lax
from jax.experimental import pallas as pl
from jax.experimental.pallas import tpu as pltpu
from jax.sharding import Mesh
from jax.sharding import PartitionSpec as P

REP = ("y", "z", "c")
CHIPS = ("y", "z")
PRECISE = lax.Precision.HIGHEST
MOMENTUM_RATE = 0.9
LEARN_RATE = 0.5
F32 = jnp.float32
BF16 = jnp.bfloat16
SWAP = ((0, 1), (1, 0))
LANES = 128
PIVOTS = 8
CHUNKS = 2
TP = 4
VMEM = pl.BlockSpec(memory_space=pltpu.VMEM)
ANY = pl.BlockSpec(memory_space=pl.ANY)
SMALL = pltpu.CompilerParams(vmem_limit_bytes=8 << 20)
PACK = pltpu.CompilerParams(vmem_limit_bytes=54400 << 10)
LARGE = pltpu.CompilerParams(vmem_limit_bytes=20 << 20)


def split(values):
    high = values.astype(BF16)
    return high, (values - high.astype(F32)).astype(BF16)


def exchange(array, axis):
    return lax.all_to_all(array, axis, 0, 0, tiled=True)


def product(left, right, dims, precision=None):
    return lax.dot_general(left, right, (dims, ((), ())), precision=precision, preferred_element_type=F32)


def times_exact(factor, exact, dims):
    both = product(jnp.concatenate(split(factor), 0), exact, dims)
    rows = factor.shape[0]
    return both[:rows] + both[rows:]


def lower_inverse(gram):
    n = gram.shape[0]
    lane = lax.broadcasted_iota(jnp.int32, (n, LANES), 1)
    row = lax.broadcasted_iota(jnp.int32, (n, LANES), 0)
    eye = jnp.where(lane == row + n, 1.0, 0.0).astype(F32)
    work = jnp.concatenate([gram, jnp.zeros((n, LANES - n), F32)], 1) + eye
    inverses = []
    for first in range(0, n, PIVOTS):
        cols = [jnp.broadcast_to(work[:, first + j : first + j + 1], (n, LANES)) for j in range(PIVOTS)]
        lines = [work[first + j : first + j + 1, :] for j in range(PIVOTS)]
        for j in range(PIVOTS):
            at = first + j
            inverse = 1.0 / cols[j][at : at + 1, :]
            inverses.append(inverse)
            scaled = lines[j] * inverse
            below = jnp.where(row > at, cols[j], 0.0)
            for m in range(j + 1, PIVOTS):
                lines[m] = lines[m] - cols[j][first + m : first + m + 1, :] * scaled
                cols[m] = cols[m] - below * (cols[m][at : at + 1, :] * inverse)
            work = work - below * scaled
    return (work * jnp.sqrt(jnp.concatenate(inverses, 0)))[:, n : 2 * n]


def gram_inverse(left):
    return lower_inverse(product(left, left, ((1,), (1,)), PRECISE))


def quarter_of(vector):
    count = vector.shape[0] // TP
    rows = [vector[lax.axis_index("tp") * count + j] for j in range(count)]
    return jnp.concatenate(rows + [jnp.zeros((8 - count, LANES), F32)], 0)


def pack_kernel(gradients, feedback, sent, kept, narrow, wide, sems):
    core = lax.axis_index("c")
    chips = gradients.shape[0]
    step = chips // CHUNKS
    spans = [slice(chunk * step, (chunk + 1) * step) for chunk in range(CHUNKS)]
    copies = []
    for chunk, span in enumerate(spans):
        pair = ((gradients, narrow), (feedback, wide))
        copies += [pltpu.make_async_copy(s.at[span], t.at[span], sems.at[chunk, w]) for w, (s, t) in enumerate(pair)]
    for copy in copies:
        copy.start()
    for chunk, span in enumerate(spans):
        copies[2 * chunk].wait()
        copies[2 * chunk + 1].wait()
        sent[span] = (narrow[span, 1 - core].astype(F32) + wide[span, 1 - core]).astype(BF16)
        kept[span] = narrow[span, core].astype(F32) + wide[span, core]


def pair_kernel(kept, received, out):
    out[...] = (kept[...] + received[...].astype(F32)).astype(BF16)


def share_kernel(arrived, vector, momentum, master, out):
    total = jnp.sum(arrived[...].astype(F32), axis=0)
    base = master[...] - LEARN_RATE * MOMENTUM_RATE * momentum[...]
    shared = jnp.concatenate([total, quarter_of(vector), base], 1).astype(BF16)
    out[...] = jnp.broadcast_to(shared, out.shape)


def matrix_of(ref, cols):
    return ref[:, :, :cols].reshape(-1, cols)


def left_kernel(near, factor, out):
    cols = factor.shape[1]
    left = times_exact(factor[...], matrix_of(near, cols), ((1,), (1,)))
    high, low = split(jnp.sum(near[:, :, cols : cols + LANES].astype(F32), axis=0))
    blank = jnp.zeros((8, left.shape[1] - 2 * LANES), F32)
    rows = jnp.concatenate([high.astype(F32), low.astype(F32), blank], 1)
    both = jnp.concatenate([left, rows], 0).astype(BF16)
    out[...] = jnp.broadcast_to(both, out.shape)


def left_sum(arrived):
    tp = arrived.shape[0] // 2
    rank = arrived.shape[1] - 8
    core = lax.axis_index("c")

    def half(side):
        return jnp.sum(arrived[pl.ds(side * tp, tp), :rank].astype(F32), axis=0)

    return half(core), half(1 - core)


def power_kernel(arrived, near, far, out):
    cols = near.shape[2] * 2 // 5
    own, other = left_sum(arrived)
    near_matrix, far_matrix = matrix_of(near, cols), matrix_of(far, cols)
    right = times_exact(own, near_matrix, ((1,), (0,))) + times_exact(other, far_matrix, ((1,), (0,)))
    half = own.shape[1]
    for side, matrix in enumerate((near_matrix, far_matrix)):
        left = times_exact(right, matrix, ((1,), (1,))).astype(BF16)
        out[:, :, side * half : (side + 1) * half] = jnp.broadcast_to(left, (out.shape[0], *left.shape))


def factor_kernel(arrived, after, out, vector):
    del after
    peers, filled = arrived.shape[:2]
    tp, rank = peers // 2, filled - 8
    count = vector.shape[0] // tp
    for column in range(tp):
        tiles = arrived[column, rank:].astype(F32) + arrived[tp + column, rank:].astype(F32)
        tile = tiles[:, :LANES] + tiles[:, LANES : 2 * LANES]
        for row in range(count):
            vector[column * count + row] = tile[row : row + 1]
    own, other = left_sum(arrived)
    out[...] = gram_inverse(jnp.concatenate([own, other], 1))


def finish_kernel(
    parts,
    inverse_one,
    near,
    far,
    gradients,
    feedback,
    momentum,
    master,
    new_feedback,
    weight,
    new_momentum,
    new_master,
    ortho_terms,
    right_terms,
    feedback_buffer,
    weight_buffer,
    base,
    owned,
    sems,
    *,
    replicas,
):
    core, chip = lax.axis_index("c"), lax.axis_index(CHIPS)
    chips, pair, cols = feedback.shape
    rows = pair // 2
    half = chips * rows
    for side, ref in ((core, near), (1 - core, far)):
        base[side] = ref[:, :, cols + LANES :]
    left = product(inverse_one[...], jnp.sum(parts[...].astype(F32), axis=0), ((1,), (0,)), PRECISE)
    ortho = product(gram_inverse(left), left, ((1,), (0,)), PRECISE)
    right = times_exact(ortho[:, :half], matrix_of(near, cols), ((1,), (0,)))
    right += times_exact(ortho[:, half:], matrix_of(far, cols), ((1,), (0,)))
    right_high, right_low = split(right / replicas)
    right_terms[...] = jnp.concatenate([right_high, right_low, right_high], 0)
    for side, start in enumerate((core * half, (1 - core) * half)):
        high, low = split(ortho[:, side * half : (side + 1) * half])
        ortho_terms[:, pl.ds(pl.multiple_of(start, LANES), half)] = jnp.concatenate([high, high, low], 0)
    for side in range(2):
        terms = ortho_terms[:, side * half : (side + 1) * half]
        owned[side] = product(terms, right_terms[...], ((0,), (0,))).reshape(chips, rows, cols)
    approx = jnp.concatenate([owned[side] for side in range(2)], 1)
    feedback_buffer[...] = gradients[...].astype(F32) + feedback[...] - approx
    copies = [pltpu.make_async_copy(feedback_buffer, new_feedback, sems.at[0])]
    copies[0].start()
    kept = jnp.concatenate([base[side].astype(F32) for side in range(2)], 1)
    weight_buffer[...] = (kept - LEARN_RATE * approx).astype(BF16)
    copies.append(pltpu.make_async_copy(weight_buffer, weight, sems.at[1]))
    copies[1].start()
    moved = MOMENTUM_RATE * momentum[...] + owned[core, chip]
    new_momentum[...] = moved
    new_master[...] = master[...] - LEARN_RATE * moved
    for copy in copies:
        copy.wait()


def shards(
    gradients,
    feedback,
    warm_factor,
    momentum,
    master_owned,
    vector_grads,
    vector_params,
    vector_momentum,
):
    replicas = lax.axis_size(REP)
    chips = lax.axis_size(CHIPS)
    tp = lax.axis_size("tp")
    rows, cols = gradients.shape[1:]
    owned = momentum.shape[0]
    rank = warm_factor.shape[1]
    half = rows // 2
    by_pair = (chips, 2 * owned, cols)
    by_owner = (chips, 2, owned, cols)
    lines = vector_grads.reshape(-1, 1, LANES)
    halves = (gradients.reshape(by_owner), feedback.reshape(by_owner))
    sent, kept = pl.pallas_call(
        pack_kernel,
        out_shape=(
            jax.ShapeDtypeStruct((chips, owned, cols), BF16),
            jax.ShapeDtypeStruct((chips, owned, cols), F32),
        ),
        in_specs=[ANY] * 2,
        out_specs=(VMEM, VMEM),
        scratch_shapes=[
            pltpu.VMEM(by_owner, BF16),
            pltpu.VMEM(by_owner, F32),
            pltpu.SemaphoreType.DMA((CHUNKS, 2)),
        ],
        compiler_params=PACK,
        name="pack",
    )(*halves)
    received = lax.ppermute(sent, "c", SWAP)
    paired = pl.pallas_call(
        pair_kernel,
        out_shape=jax.ShapeDtypeStruct((chips, owned, cols), BF16),
        in_specs=[VMEM] * 2,
        out_specs=VMEM,
        compiler_params=SMALL,
        name="pair",
    )(kept, received)
    arrived = exchange(paired, CHIPS)

    shared_cols = 2 * cols + LANES
    shared = pl.pallas_call(
        share_kernel,
        out_shape=jax.ShapeDtypeStruct((chips, owned, shared_cols), BF16),
        in_specs=[VMEM] * 4,
        out_specs=VMEM,
        compiler_params=SMALL,
        name="share",
    )(arrived, lines, momentum, master_owned)
    near = exchange(shared, CHIPS)
    far = lax.ppermute(near, "c", SWAP)
    left = pl.pallas_call(
        left_kernel,
        out_shape=jax.ShapeDtypeStruct((2 * tp, rank + 8, half), BF16),
        in_specs=[VMEM] * 2,
        out_specs=VMEM,
        compiler_params=SMALL,
        name="left",
    )(near, warm_factor.T)
    left = exchange(left, ("c", "tp"))
    parts = pl.pallas_call(
        power_kernel,
        out_shape=jax.ShapeDtypeStruct((tp, rank, rows), BF16),
        in_specs=[VMEM] * 3,
        out_specs=VMEM,
        compiler_params=SMALL,
        name="power",
    )(left, near, far)
    inverse_one, vector = pl.pallas_call(
        factor_kernel,
        out_shape=(jax.ShapeDtypeStruct((rank, rank), F32), jax.ShapeDtypeStruct(lines.shape, F32)),
        in_specs=[VMEM, ANY],
        out_specs=(VMEM, VMEM),
        compiler_params=SMALL,
        name="factor",
    )(left, parts)
    parts = exchange(parts, "tp")
    vector_sum = vector.reshape(-1)

    new_feedback, weight, new_momentum, new_master = pl.pallas_call(
        functools.partial(finish_kernel, replicas=replicas),
        out_shape=(
            jax.ShapeDtypeStruct(by_pair, F32),
            jax.ShapeDtypeStruct(by_pair, BF16),
            jax.ShapeDtypeStruct(momentum.shape, F32),
            jax.ShapeDtypeStruct(momentum.shape, F32),
        ),
        in_specs=[VMEM] * 8,
        out_specs=(ANY, ANY, VMEM, VMEM),
        scratch_shapes=[
            pltpu.VMEM((3 * rank, rows), BF16),
            pltpu.VMEM((3 * rank, cols), BF16),
            pltpu.VMEM(by_pair, F32),
            pltpu.VMEM(by_pair, BF16),
            pltpu.VMEM((2, chips, owned, cols), BF16),
            pltpu.VMEM((2, chips, owned, cols), F32),
            pltpu.SemaphoreType.DMA((2,)),
        ],
        compiler_params=LARGE,
        name="finish",
    )(
        parts,
        inverse_one,
        near,
        far,
        gradients.reshape(by_pair),
        feedback.reshape(by_pair),
        momentum,
        master_owned,
    )
    new_vector_momentum = MOMENTUM_RATE * vector_momentum + vector_sum / replicas
    new_vector_params = vector_params - LEARN_RATE * new_vector_momentum
    return (
        new_feedback.reshape(feedback.shape),
        new_momentum,
        new_master,
        weight.reshape(rows, cols),
        new_vector_params,
        new_vector_momentum,
    )


def solution(mesh):
    finer = Mesh(mesh.devices.reshape(8, 8, 2, mesh.shape["tp"]), ("y", "z", "c", "tp"))
    in_specs = (
        P(REP, None, "tp"),
        P(REP, None, "tp"),
        P("tp", None),
        P(REP, "tp"),
        P(REP, "tp"),
        P(REP, None),
        P(),
        P(),
    )
    out_specs = (P(REP, None, "tp"), P(REP, "tp"), P(REP, "tp"), P(None, "tp"), P(), P())
    return jax.shard_map(
        shards, mesh=finer, in_specs=in_specs, out_specs=out_specs, check_vma=False
    )
```

```python
import functools

import jax
import jax.numpy as jnp
from jax import lax
from jax.experimental import pallas as pl
from jax.experimental.pallas import tpu as pltpu
from jax.sharding import Mesh
from jax.sharding import PartitionSpec as P

REP = ("y", "z", "c")
CHIPS = ("y", "z")
PRECISE = lax.Precision.HIGHEST
MOMENTUM_RATE = 0.9
LEARN_RATE = 0.5
F32 = jnp.float32
BF16 = jnp.bfloat16
SWAP = ((0, 1), (1, 0))
LANES = 128
PIVOTS = 8
CHUNKS = 2
TP = 4
VMEM = pl.BlockSpec(memory_space=pltpu.VMEM)
ANY = pl.BlockSpec(memory_space=pl.ANY)
SMALL = pltpu.CompilerParams(vmem_limit_bytes=8 << 20)
PACK = pltpu.CompilerParams(vmem_limit_bytes=54400 << 10)
LARGE = pltpu.CompilerParams(vmem_limit_bytes=20 << 20)


def split(values):
    high = values.astype(BF16)
    return high, (values - high.astype(F32)).astype(BF16)


def exchange(array, axis):
    return lax.all_to_all(array, axis, 0, 0, tiled=True)


def product(left, right, dims, precision=None):
    return lax.dot_general(left, right, (dims, ((), ())), precision=precision, preferred_element_type=F32)


def times_exact(factor, exact, dims):
    both = product(jnp.concatenate(split(factor), 0), exact, dims)
    rows = factor.shape[0]
    return both[:rows] + both[rows:]


def lower_inverse(gram):
    n = gram.shape[0]
    lane = lax.broadcasted_iota(jnp.int32, (n, LANES), 1)
    row = lax.broadcasted_iota(jnp.int32, (n, LANES), 0)
    eye = jnp.where(lane == row + n, 1.0, 0.0).astype(F32)
    work = jnp.concatenate([gram, jnp.zeros((n, LANES - n), F32)], 1) + eye
    inverses = []
    for first in range(0, n, PIVOTS):
        cols = [jnp.broadcast_to(work[:, first + j : first + j + 1], (n, LANES)) for j in range(PIVOTS)]
        lines = [work[first + j : first + j + 1, :] for j in range(PIVOTS)]
        for j in range(PIVOTS):
            at = first + j
            inverse = 1.0 / cols[j][at : at + 1, :]
            inverses.append(inverse)
            scaled = lines[j] * inverse
            below = jnp.where(row > at, cols[j], 0.0)
            for m in range(j + 1, PIVOTS):
                lines[m] = lines[m] - cols[j][first + m : first + m + 1, :] * scaled
                cols[m] = cols[m] - below * (cols[m][at : at + 1, :] * inverse)
            work = work - below * scaled
    return (work * jnp.sqrt(jnp.concatenate(inverses, 0)))[:, n : 2 * n]


def gram_inverse(left):
    return lower_inverse(product(left, left, ((1,), (1,)), PRECISE))


def quarter_of(vector):
    count = vector.shape[0] // TP
    rows = [vector[lax.axis_index("tp") * count + j] for j in range(count)]
    return jnp.concatenate(rows + [jnp.zeros((8 - count, LANES), F32)], 0)


def pack_kernel(gradients, feedback, sent, kept, narrow, wide, sems):
    core = lax.axis_index("c")
    chips = gradients.shape[0]
    step = chips // CHUNKS
    spans = [slice(chunk * step, (chunk + 1) * step) for chunk in range(CHUNKS)]
    copies = []
    for chunk, span in enumerate(spans):
        pair = ((gradients, narrow), (feedback, wide))
        copies += [pltpu.make_async_copy(s.at[span], t.at[span], sems.at[chunk, w]) for w, (s, t) in enumerate(pair)]
    for copy in copies:
        copy.start()
    for chunk, span in enumerate(spans):
        copies[2 * chunk].wait()
        copies[2 * chunk + 1].wait()
        sent[span] = (narrow[span, 1 - core].astype(F32) + wide[span, 1 - core]).astype(BF16)
        kept[span] = narrow[span, core].astype(F32) + wide[span, core]


def pair_kernel(kept, received, out):
    out[...] = (kept[...] + received[...].astype(F32)).astype(BF16)


def share_kernel(arrived, vector, momentum, master, out):
    total = jnp.sum(arrived[...].astype(F32), axis=0)
    base = master[...] - LEARN_RATE * MOMENTUM_RATE * momentum[...]
    shared = jnp.concatenate([total, quarter_of(vector), base], 1).astype(BF16)
    out[...] = jnp.broadcast_to(shared, out.shape)


def matrix_of(ref, cols):
    return ref[:, :, :cols].reshape(-1, cols)


def left_kernel(near, factor, out):
    cols = factor.shape[1]
    left = times_exact(factor[...], matrix_of(near, cols), ((1,), (1,)))
    high, low = split(jnp.sum(near[:, :, cols : cols + LANES].astype(F32), axis=0))
    blank = jnp.zeros((8, left.shape[1] - 2 * LANES), F32)
    rows = jnp.concatenate([high.astype(F32), low.astype(F32), blank], 1)
    both = jnp.concatenate([left, rows], 0).astype(BF16)
    out[...] = jnp.broadcast_to(both, out.shape)


def left_sum(arrived):
    tp = arrived.shape[0] // 2
    rank = arrived.shape[1] - 8
    core = lax.axis_index("c")

    def half(side):
        return jnp.sum(arrived[pl.ds(side * tp, tp), :rank].astype(F32), axis=0)

    return half(core), half(1 - core)


def power_kernel(arrived, near, far, out):
    cols = near.shape[2] * 2 // 5
    own, other = left_sum(arrived)
    near_matrix, far_matrix = matrix_of(near, cols), matrix_of(far, cols)
    right = times_exact(own, near_matrix, ((1,), (0,))) + times_exact(other, far_matrix, ((1,), (0,)))
    half = own.shape[1]
    for side, matrix in enumerate((near_matrix, far_matrix)):
        left = times_exact(right, matrix, ((1,), (1,))).astype(BF16)
        out[:, :, side * half : (side + 1) * half] = jnp.broadcast_to(left, (out.shape[0], *left.shape))


def factor_kernel(arrived, after, out, vector):
    del after
    peers, filled = arrived.shape[:2]
    tp, rank = peers // 2, filled - 8
    count = vector.shape[0] // tp
    for column in range(tp):
        tiles = arrived[column, rank:].astype(F32) + arrived[tp + column, rank:].astype(F32)
        tile = tiles[:, :LANES] + tiles[:, LANES : 2 * LANES]
        for row in range(count):
            vector[column * count + row] = tile[row : row + 1]
    own, other = left_sum(arrived)
    out[...] = gram_inverse(jnp.concatenate([own, other], 1))


def finish_kernel(
    parts,
    inverse_one,
    near,
    far,
    far_base,
    gradients,
    feedback,
    momentum,
    master,
    new_feedback,
    weight,
    new_momentum,
    new_master,
    ortho_terms,
    right_terms,
    feedback_buffer,
    weight_buffer,
    base,
    owned,
    sems,
    *,
    replicas,
):
    core, chip = lax.axis_index("c"), lax.axis_index(CHIPS)
    chips, pair, cols = feedback.shape
    rows = pair // 2
    half = chips * rows
    base[core] = near[:, :, cols + LANES :]
    base[1 - core] = far_base[...]
    left = product(inverse_one[...], jnp.sum(parts[...].astype(F32), axis=0), ((1,), (0,)), PRECISE)
    ortho = product(gram_inverse(left), left, ((1,), (0,)), PRECISE)
    right = times_exact(ortho[:, :half], matrix_of(near, cols), ((1,), (0,)))
    right += times_exact(ortho[:, half:], matrix_of(far, cols), ((1,), (0,)))
    right_high, right_low = split(right / replicas)
    right_terms[...] = jnp.concatenate([right_high, right_low, right_high], 0)
    for side, start in enumerate((core * half, (1 - core) * half)):
        high, low = split(ortho[:, side * half : (side + 1) * half])
        ortho_terms[:, pl.ds(pl.multiple_of(start, LANES), half)] = jnp.concatenate([high, high, low], 0)
    for side in range(2):
        terms = ortho_terms[:, side * half : (side + 1) * half]
        owned[side] = product(terms, right_terms[...], ((0,), (0,))).reshape(chips, rows, cols)
    approx = jnp.concatenate([owned[side] for side in range(2)], 1)
    feedback_buffer[...] = gradients[...].astype(F32) + feedback[...] - approx
    copies = [pltpu.make_async_copy(feedback_buffer, new_feedback, sems.at[0])]
    copies[0].start()
    kept = jnp.concatenate([base[side].astype(F32) for side in range(2)], 1)
    weight_buffer[...] = (kept - LEARN_RATE * approx).astype(BF16)
    copies.append(pltpu.make_async_copy(weight_buffer, weight, sems.at[1]))
    copies[1].start()
    moved = MOMENTUM_RATE * momentum[...] + owned[core, chip]
    new_momentum[...] = moved
    new_master[...] = master[...] - LEARN_RATE * moved
    for copy in copies:
        copy.wait()


def shards(
    gradients,
    feedback,
    warm_factor,
    momentum,
    master_owned,
    vector_grads,
    vector_params,
    vector_momentum,
):
    replicas = lax.axis_size(REP)
    chips = lax.axis_size(CHIPS)
    tp = lax.axis_size("tp")
    rows, cols = gradients.shape[1:]
    owned = momentum.shape[0]
    rank = warm_factor.shape[1]
    half = rows // 2
    by_pair = (chips, 2 * owned, cols)
    by_owner = (chips, 2, owned, cols)
    lines = vector_grads.reshape(-1, 1, LANES)
    halves = (gradients.reshape(by_owner), feedback.reshape(by_owner))
    sent, kept = pl.pallas_call(
        pack_kernel,
        out_shape=(
            jax.ShapeDtypeStruct((chips, owned, cols), BF16),
            jax.ShapeDtypeStruct((chips, owned, cols), F32),
        ),
        in_specs=[ANY] * 2,
        out_specs=(VMEM, VMEM),
        scratch_shapes=[
            pltpu.VMEM(by_owner, BF16),
            pltpu.VMEM(by_owner, F32),
            pltpu.SemaphoreType.DMA((CHUNKS, 2)),
        ],
        compiler_params=PACK,
        name="pack",
    )(*halves)
    received = lax.ppermute(sent, "c", SWAP)
    paired = pl.pallas_call(
        pair_kernel,
        out_shape=jax.ShapeDtypeStruct((chips, owned, cols), BF16),
        in_specs=[VMEM] * 2,
        out_specs=VMEM,
        compiler_params=SMALL,
        name="pair",
    )(kept, received)
    arrived = exchange(paired, CHIPS)

    shared_cols = 2 * cols + LANES
    shared = pl.pallas_call(
        share_kernel,
        out_shape=jax.ShapeDtypeStruct((chips, owned, shared_cols), BF16),
        in_specs=[VMEM] * 4,
        out_specs=VMEM,
        compiler_params=SMALL,
        name="share",
    )(arrived, lines, momentum, master_owned)
    near = exchange(shared, CHIPS)
    far = lax.ppermute(near[:, :, :cols], "c", SWAP)
    left = pl.pallas_call(
        left_kernel,
        out_shape=jax.ShapeDtypeStruct((2 * tp, rank + 8, half), BF16),
        in_specs=[VMEM] * 2,
        out_specs=VMEM,
        compiler_params=SMALL,
        name="left",
    )(near, warm_factor.T)
    left = exchange(left, ("c", "tp"))
    parts = pl.pallas_call(
        power_kernel,
        out_shape=jax.ShapeDtypeStruct((tp, rank, rows), BF16),
        in_specs=[VMEM] * 3,
        out_specs=VMEM,
        compiler_params=SMALL,
        name="power",
    )(left, near, far)
    inverse_one, vector = pl.pallas_call(
        factor_kernel,
        out_shape=(jax.ShapeDtypeStruct((rank, rank), F32), jax.ShapeDtypeStruct(lines.shape, F32)),
        in_specs=[VMEM, ANY],
        out_specs=(VMEM, VMEM),
        compiler_params=SMALL,
        name="factor",
    )(left, parts)
    parts = exchange(parts, "tp")
    far_base = lax.ppermute(near[:, :, cols + LANES :], "c", SWAP)
    vector_sum = vector.reshape(-1)

    new_feedback, weight, new_momentum, new_master = pl.pallas_call(
        functools.partial(finish_kernel, replicas=replicas),
        out_shape=(
            jax.ShapeDtypeStruct(by_pair, F32),
            jax.ShapeDtypeStruct(by_pair, BF16),
            jax.ShapeDtypeStruct(momentum.shape, F32),
            jax.ShapeDtypeStruct(momentum.shape, F32),
        ),
        in_specs=[VMEM] * 9,
        out_specs=(ANY, ANY, VMEM, VMEM),
        scratch_shapes=[
            pltpu.VMEM((3 * rank, rows), BF16),
            pltpu.VMEM((3 * rank, cols), BF16),
            pltpu.VMEM(by_pair, F32),
            pltpu.VMEM(by_pair, BF16),
            pltpu.VMEM((2, chips, owned, cols), BF16),
            pltpu.VMEM((2, chips, owned, cols), F32),
            pltpu.SemaphoreType.DMA((2,)),
        ],
        compiler_params=LARGE,
        name="finish",
    )(
        parts,
        inverse_one,
        near,
        far,
        far_base,
        gradients.reshape(by_pair),
        feedback.reshape(by_pair),
        momentum,
        master_owned,
    )
    new_vector_momentum = MOMENTUM_RATE * vector_momentum + vector_sum / replicas
    new_vector_params = vector_params - LEARN_RATE * new_vector_momentum
    return (
        new_feedback.reshape(feedback.shape),
        new_momentum,
        new_master,
        weight.reshape(rows, cols),
        new_vector_params,
        new_vector_momentum,
    )


def solution(mesh):
    finer = Mesh(mesh.devices.reshape(8, 8, 2, mesh.shape["tp"]), ("y", "z", "c", "tp"))
    in_specs = (
        P(REP, None, "tp"),
        P(REP, None, "tp"),
        P("tp", None),
        P(REP, "tp"),
        P(REP, "tp"),
        P(REP, None),
        P(),
        P(),
    )
    out_specs = (P(REP, None, "tp"), P(REP, "tp"), P(REP, "tp"), P(None, "tp"), P(), P())
    return jax.shard_map(
        shards, mesh=finer, in_specs=in_specs, out_specs=out_specs, check_vma=False
    )
```
